32 devices in a mesh: chan: 8 (over z, y), win: 4 (over x, core).
Axes of the slice: x: 2, y: 2, z: 4, core: 2. Of those that a mesh axis runs over, the one named last changes fastest.
Arguments:
- samples: bfloat16 [8, 256, 6144], P('win', 'chan'), may hold values from -6 to 6
- pair_offsets: int32 [8, 3], P('chan'), may hold values from 0 to 2, each once within a row
- spectral_slot_position: int32 [1024], replicated, may hold values from 1 to 3071, as said below
Outputs:
- correlations: float32 [256, 3, 2, 32, 1024], P('chan', None, None, None, 'win')
The draws below stay inside these ranges and needn't reach their ends.
Inputs may be any that keep to these rules, and one draw needn't show every extreme that they name: `pair_offsets`: each row holds every offset of 0 to 2 once. `spectral_slot_position`: distinct and rising; the first is 1 and the last is 3071.
All inputs are finite; a program needn't handle non-finite values.
Results may differ from the reference program's by a relative error of at most 0.0036.
Values sent between devices are 32-bit elements; how exact they have to be, the bound alone decides.
No kernel may reach another device: no remote copies, remote signals or barrier semaphores. Data moves between devices by JAX's collectives and lax.ppermute only.
A program may use at most 64 MiB of HBM per device.

```python
import math
import jax
import jax.numpy as jnp
from jax import lax

CB = 32
S = 6144
F = 1024
HALF = 64
TB = 1024
NPART = 3
BLOCKS = 8
CHANNELS = 256
WINDOWS = 8


def draw_spectral_slot_position(key, part):
    inner = jax.random.permutation(key, S // 2 - 3).astype(jnp.int32) + 2
    chosen = inner[:F - 2]
    ends = jnp.array([1, S // 2 - 1], jnp.int32)
    return jnp.sort(jnp.concatenate([chosen, ends])).astype(jnp.int32)


def steps_of(key, dims, split, smallest, top_value):
    def one(dim, shards_of):
        steps = jax.random.uniform(jax.random.fold_in(jax.random.fold_in(key, 6), dim), (shards_of,), jnp.float32, smallest / len(split), top_value / len(split))
        return jnp.repeat(jnp.exp(steps), dims[dim] // shards_of).reshape((-1,) + (1,) * (len(dims) - dim - 1))

    loudness = one(*split[0])
    for cut in split[1:]:
        loudness = loudness * one(*cut)
    return loudness


def normal_values(stream_key, shape, scale, reach, shards=(), held_as=jnp.bfloat16):
    factor_of = steps_of(stream_key, shape, shards, -0.22, 0.18) if shards else 1.0
    drawn = jax.random.normal(stream_key, shape, jnp.float32) * scale * factor_of
    return jnp.minimum(jnp.maximum(drawn, -reach), reach).astype(held_as)


def setup_inputs(seed: int = 0) -> dict:
    streams_of = jax.random.split(jax.random.key(seed), 4)
    samples = normal_values(streams_of[0], (WINDOWS, CHANNELS, S), 1.0, 6.0, ((0, 4), (1, 8)))
    pair_offsets = jax.vmap(lambda own: jax.random.permutation(own, NPART))(jax.random.split(streams_of[1], BLOCKS)).reshape((BLOCKS, NPART)).astype(jnp.int32)
    spectral_slot_position = draw_spectral_slot_position(jax.random.fold_in(streams_of[3], 71), 0)
    return {"samples": samples, "pair_offsets": pair_offsets, "spectral_slot_position": spectral_slot_position}


EPSILON = 1e-06

def angle_parts(spectral_slot_position):
    factor = 2.0 * math.pi / S
    moments = jnp.arange(TB, dtype=jnp.int32)
    base = (moments[:, None] * spectral_slot_position[None, :] % S).astype(jnp.float32) * factor
    starts = jnp.arange(S // TB, dtype=jnp.int32) * TB
    turns = (starts[:, None] * spectral_slot_position[None, :] % S).astype(jnp.float32) * factor
    return (jnp.cos(base), jnp.sin(base), jnp.cos(turns), jnp.sin(turns))

def block_table(base_cos, base_sin, turn_cos, turn_sin):
    scale = 1.0 / math.sqrt(S)
    cos_part = (base_cos * turn_cos - base_sin * turn_sin) * scale
    sin_part = (base_sin * turn_cos + base_cos * turn_sin) * scale
    return jnp.concatenate([cos_part, sin_part], axis=-1).astype(jnp.bfloat16)

def whiten(spectra, half_width):
    freq_count = spectra.shape[-1]
    powers = spectra[..., 0, :] * spectra[..., 0, :] + spectra[..., 1, :] * spectra[..., 1, :]
    places = jnp.arange(freq_count, dtype=jnp.int32)
    banded = (jnp.abs(places[:, None] - places[None, :]) <= half_width).astype(jnp.float32)
    tallies = lax.optimization_barrier(jnp.sum(banded, axis=0))
    flattened = powers.reshape(-1, freq_count)
    smoothed_amplitude = jnp.dot(flattened, banded, precision=lax.Precision.HIGHEST).reshape(powers.shape) / tallies
    amplitude = jnp.sqrt(smoothed_amplitude + EPSILON)
    return spectra / amplitude[..., None, :]

def correlate(mine, partner, windows):
    highest = lax.Precision.HIGHEST

    def product(left, right):
        return jnp.einsum('wif,wjf->ijf', left, right, precision=highest)
    real_part = (product(mine[:, :, 0], partner[:, :, 0]) + product(mine[:, :, 1], partner[:, :, 1])) / windows
    imag_part = (product(mine[:, :, 1], partner[:, :, 0]) - product(mine[:, :, 0], partner[:, :, 1])) / windows
    return jnp.stack([real_part, imag_part], axis=1)

def reference(samples, pair_offsets, spectral_slot_position):
    base_cos, base_sin, turn_cos, turn_sin = angle_parts(spectral_slot_position)
    table = block_table(base_cos[None, :, :], base_sin[None, :, :], turn_cos[:, None, :], turn_sin[:, None, :])
    table = table.reshape(S, 2 * F).astype(jnp.float32)

    def transform(window):
        return jnp.dot(window.astype(jnp.float32), table, precision=lax.Precision.HIGHEST)
    raw_parts = lax.map(transform, samples)
    spectra = jnp.stack([raw_parts[..., :F], -raw_parts[..., F:]], axis=2)
    whitened = whiten(spectra, HALF)
    grouped = whitened.reshape(WINDOWS, BLOCKS, CB, 2, F).transpose(1, 0, 2, 3, 4)
    padded = jnp.concatenate([jnp.zeros((2,) + grouped.shape[1:], jnp.float32), grouped], axis=0)

    def one_block(inputs):
        index, offsets = inputs
        mine = lax.dynamic_index_in_dim(padded, index + 2, 0, keepdims=False)
        stacks = []
        for position in range(NPART):
            partner = lax.dynamic_index_in_dim(padded, index + 2 - offsets[position], 0, keepdims=False)
            stacks.append(correlate(mine, partner, WINDOWS))
        return jnp.stack(stacks, axis=1)
    result = lax.map(one_block, (jnp.arange(BLOCKS, dtype=jnp.int32), pair_offsets))
    return result.reshape(CHANNELS, NPART, 2, CB, F)
```

```python
import functools
import math

import jax
import jax.numpy as jnp
import numpy as np
from jax import lax
from jax.experimental import pallas as pl
from jax.experimental.pallas import tpu as pltpu
from jax.sharding import PartitionSpec as P

HALF = 64
EPSILON = 1e-06
LANES = 128


def turned(value, numerator, denominator):
    real, imag = value
    numerator %= denominator
    if numerator == 0:
        return value
    if 2 * numerator == denominator:
        return (-real, None if imag is None else -imag)
    if 4 * numerator == denominator:
        return (imag, -real)
    if 4 * numerator == 3 * denominator:
        return (None if imag is None else -imag, real)
    c = math.cos(2 * math.pi * numerator / denominator)
    s = math.sin(2 * math.pi * numerator / denominator)
    if imag is None:
        return (real * c, real * (-s))
    return (real * c + imag * s, imag * c - real * s)


def plus(left, right):
    return tuple(b if a is None else a if b is None else a + b for a, b in zip(left, right))


def minus(left, right):
    return tuple(
        (None if b is None else -b) if a is None else a if b is None else a - b
        for a, b in zip(left, right)
    )


def scaled(value, factor):
    return tuple(None if a is None else a * factor for a in value)


def flipped(value):
    return (value[0], None if value[1] is None else -value[1])


def real_transform(count, first, stride, load):
    if count == 1:
        return [(load(first), None)]
    radix = 2 if count % 2 == 0 and count % 3 else 3 if count % 3 == 0 else count
    if radix == 2:
        part = count // 2
        even = real_transform(part, first, stride * 2, load)
        odd = real_transform(part, first + stride, stride * 2, load)
        bins = [None] * (count // 2 + 1)
        for k in range(part // 2 + 1):
            turn = turned(odd[k], k, count)
            bins[k] = plus(even[k], turn)
            if part - k != k:
                bins[part - k] = flipped(minus(even[k], turn))
        return bins
    if radix == 3:
        part = count // 3
        zero, one, two = (real_transform(part, first + stride * n, stride * 3, load) for n in range(3))
        bins = [None] * (count // 2 + 1)

        def keep(place, value):
            place %= count
            if place > count // 2:
                place, value = count - place, flipped(value)
            if bins[place] is None:
                bins[place] = value

        for k in range(part // 2 + 1):
            a, b = turned(one[k], k, count), turned(two[k], 2 * k, count)
            total, gap = plus(a, b), scaled(minus(a, b), math.sqrt(3.0) / 2)
            keep(k, plus(zero[k], total))
            middle = minus(zero[k], scaled(total, 0.5))
            side = turned(gap, 1, 4)
            keep(k + part, plus(middle, side))
            keep(k + 2 * part, minus(middle, side))
        return bins
    bins = []
    values = [(load(first + stride * n), None) for n in range(count)]
    for k in range(count // 2 + 1):
        bins.append(functools.reduce(plus, (turned(v, n * k, count) for n, v in enumerate(values))))
    return bins


def halves(value):
    high = value.astype(jnp.bfloat16)
    return high, (value - high.astype(jnp.float32)).astype(jnp.bfloat16)


@functools.lru_cache
def tables(span, half_width):
    outer = span // LANES
    lane = np.arange(LANES)
    turn = 2 * np.pi * np.outer(np.arange(outer // 2 + 1), lane) / span
    twiddles = np.stack([np.cos(turn), -np.sin(turn)], axis=1) / math.sqrt(span)
    inner = 2 * np.pi * (np.outer(lane, lane) % LANES) / LANES
    c, s = np.cos(inner), np.sin(inner)
    matrix = np.block([[c, -s], [s, c]]).astype(np.float32)
    high = matrix.astype(jnp.bfloat16)
    low = (matrix - high.astype(np.float32)).astype(jnp.bfloat16)
    gap = np.arange(4 * LANES)[:, None] - LANES - np.arange(2 * LANES)[None, :]
    band = (np.abs(gap) <= half_width).astype(jnp.bfloat16)
    return (
        twiddles.reshape(-1, LANES).astype(np.float32),
        np.stack([high, low]),
        band,
    )


def spectra_kernel(half_width, slab_count, place_ref, slot_ref, sample_ref, twiddle_ref, matrix_ref,
                   band_ref, *rest):
    out_refs = rest[:slab_count]
    high_ref, low_ref, fine_ref, spec_ref, power_ref = rest[slab_count:]
    windows, sensors, span = sample_ref.shape
    rows = windows * sensors
    freqs = slot_ref.shape[1]
    outer = span // LANES
    bins = outer // 2 + 1
    group = 16

    def outer_transform(step, carry):
        window = step // (sensors // group)
        start = pl.multiple_of((step % (sensors // group)) * group, group)
        first = pl.multiple_of(step * group, group)

        def load(place):
            piece = sample_ref[window, pl.ds(start, group), place * LANES:(place + 1) * LANES]
            return piece.astype(jnp.float32)

        for k, (real, imag) in enumerate(real_transform(outer, 0, 1, load)):
            c, s = twiddle_ref[2 * k:2 * k + 1, :], twiddle_ref[2 * k + 1:2 * k + 2, :]
            if imag is None:
                pair = (real * c, real * s)
            else:
                pair = (real * c - imag * s, real * s + imag * c)
            for part in range(2):
                high, low = halves(pair[part])
                high_ref[k, pl.ds(first, group), part * LANES:(part + 1) * LANES] = high
                low_ref[k, pl.ds(first, group), part * LANES:(part + 1) * LANES] = low
        return carry

    lax.fori_loop(0, rows // group, outer_transform, 0)

    high = high_ref[...].reshape(bins * rows, 2 * LANES)
    low = low_ref[...].reshape(bins * rows, 2 * LANES)
    fine = jnp.dot(high, matrix_ref[0], preferred_element_type=jnp.float32)
    fine += jnp.dot(low, matrix_ref[0], preferred_element_type=jnp.float32)
    fine += jnp.dot(high, matrix_ref[1], preferred_element_type=jnp.float32)
    fine_ref[...] = fine.reshape(bins, rows, 2 * LANES)

    def choose(block, carry):
        columns = pl.ds(pl.multiple_of(block * LANES, LANES), LANES)
        slot = slot_ref[:, columns].astype(jnp.float32)
        quotient = jnp.floor((slot + 0.5) * (1.0 / outer))
        remainder = slot - quotient * outer
        mirrored = remainder > outer // 2
        lane = jnp.where(mirrored, LANES - 1 - quotient, quotient).astype(jnp.int32)
        bin_index = jnp.where(mirrored, outer - remainder, remainder).astype(jnp.int32)
        lane = jnp.broadcast_to(lane, (8, LANES))
        bin_index = jnp.broadcast_to(bin_index, (8, LANES))
        sign = jnp.broadcast_to(jnp.where(mirrored, -1.0, 1.0), (8, LANES))
        chosen = [[jnp.zeros((8, LANES), jnp.float32)] * 2 for _ in range(rows // 8)]
        for k in range(bins):
            here = bin_index == k
            for r in range(rows // 8):
                for part in range(2):
                    piece = fine_ref[k, r * 8:(r + 1) * 8, part * LANES:(part + 1) * LANES]
                    moved = jnp.take_along_axis(piece, lane, axis=1)
                    chosen[r][part] = jnp.where(here, moved, chosen[r][part])
        for r in range(rows // 8):
            real, imag = chosen[r][0], chosen[r][1] * sign
            spec_ref[0, r * 8:(r + 1) * 8, columns] = real
            spec_ref[1, r * 8:(r + 1) * 8, columns] = imag
            power_ref[r * 8:(r + 1) * 8, columns] = real * real + imag * imag
        return carry

    lax.fori_loop(0, freqs // LANES, choose, 0)

    high, low = halves(power_ref[...])
    both = jnp.concatenate([high, low], axis=0)
    width = 2 * LANES
    place = place_ref[0]
    slab = freqs // slab_count
    smooth = []
    for c in range(freqs // width):
        first, last = max(0, c * width - LANES), min(freqs, (c + 1) * width + LANES)
        offset = first - (c * width - LANES)
        total = jnp.dot(both[:, first:last], band_ref[offset:offset + last - first, :],
                        preferred_element_type=jnp.float32)
        total = total[:rows] + total[rows:]
        spot = lax.broadcasted_iota(jnp.int32, (1, width), 1) + c * width
        tally = jnp.minimum(spot + half_width, freqs - 1) - jnp.maximum(spot - half_width, 0) + 1
        factor = lax.rsqrt(total / tally.astype(jnp.float32) + EPSILON)
        for part in range(2):
            spec_ref[part, :, c * width:(c + 1) * width] *= factor
    for turn, out_ref in enumerate(out_refs):
        columns = pl.ds(pl.multiple_of((place ^ turn) * slab, LANES), slab)
        for window in range(windows):
            for part in range(2):
                out_ref[window, part] = spec_ref[part, window * sensors:(window + 1) * sensors, columns]


def whitened_slabs(samples, slots, place, slab_count):
    windows, sensors, span = samples.shape
    freqs = slots.shape[0]
    rows = windows * sensors
    bins = span // LANES // 2 + 1
    twiddles, matrix, band = tables(span, HALF)
    whole = pl.BlockSpec(memory_space=pltpu.VMEM)
    return pl.pallas_call(
        functools.partial(spectra_kernel, HALF, slab_count),
        out_shape=[
            jax.ShapeDtypeStruct((windows, 2, sensors, freqs // slab_count), jnp.float32)
        ] * slab_count,
        in_specs=[pl.BlockSpec(memory_space=pltpu.SMEM)] + [whole] * 5,
        out_specs=[whole] * slab_count,
        scratch_shapes=[
            pltpu.VMEM((bins, rows, 2 * LANES), jnp.bfloat16),
            pltpu.VMEM((bins, rows, 2 * LANES), jnp.bfloat16),
            pltpu.VMEM((bins, rows, 2 * LANES), jnp.float32),
            pltpu.VMEM((2, rows, freqs), jnp.float32),
            pltpu.VMEM((rows, freqs), jnp.float32),
        ],
        name="whitened_slabs",
    )(place, slots.reshape(1, freqs), samples, jnp.asarray(twiddles), jnp.asarray(matrix), jnp.asarray(band))


def correlate_kernel(count, scale, slot_ref, *rest):
    mine, partner = rest[:count], rest[count:2 * count]
    out_ref = rest[-1]
    block, _, _, sensors, freqs = out_ref.shape
    windows = mine[0].shape[0]
    base = pl.program_id(0) * block
    width = 2 * LANES

    def one(step, carry):
        for c in range(freqs // width):
            columns = slice(c * width, (c + 1) * width)
            left = []
            for ref in mine:
                for w in range(windows):
                    left.append([
                        jnp.broadcast_to(ref[w, p, pl.ds(base + step, 1), columns] * scale, (8, width))
                        for p in range(2)
                    ])
            for g in range(sensors // 8):
                real = imag = None
                for n, ref in enumerate(partner):
                    for w in range(windows):
                        ar, ai = left[n * windows + w]
                        pr = ref[w, 0, g * 8:(g + 1) * 8, columns]
                        pi = ref[w, 1, g * 8:(g + 1) * 8, columns]
                        more_real, more_imag = ar * pr + ai * pi, ai * pr - ar * pi
                        real = more_real if real is None else real + more_real
                        imag = more_imag if imag is None else imag + more_imag
                out_ref[step, 0, 0, g * 8:(g + 1) * 8, columns] = real
                out_ref[step, 0, 1, g * 8:(g + 1) * 8, columns] = imag
        return carry

    lax.fori_loop(0, block, one, 0)


def correlated(slot, mine, partner, scale, earlier, slots):
    windows, _, sensors, freqs = mine[0].shape
    block = 4 if sensors % 4 == 0 else 1
    count = len(mine)
    whole = pl.BlockSpec(mine[0].shape, lambda i, slot: (0, 0, 0, 0))
    out_shape = jax.ShapeDtypeStruct((sensors, slots, 2, sensors, freqs), jnp.float32)
    operands = list(mine) + list(partner)
    in_specs = [whole] * len(operands)
    aliases = {}
    if earlier is not None:
        aliases = {1 + len(operands): 0}
        operands.append(earlier)
        in_specs.append(pl.BlockSpec(memory_space=pl.ANY))
    return pl.pallas_call(
        functools.partial(correlate_kernel, count, scale),
        out_shape=out_shape,
        grid_spec=pltpu.PrefetchScalarGridSpec(
            num_scalar_prefetch=1,
            grid=(sensors // block,),
            in_specs=in_specs,
            out_specs=pl.BlockSpec(
                (block, 1, 2, sensors, freqs), lambda i, slot: (i, slot[0], 0, 0, 0)
            ),
        ),
        input_output_aliases=aliases,
        cost_estimate=pl.CostEstimate(
            flops=8 * count * windows * sensors * sensors * freqs,
            bytes_accessed=8 * sensors * sensors * freqs,
            transcendentals=0,
        ),
        name="correlated",
    )(slot, *operands)


def passed_along(value, axis, steps):
    count = lax.axis_size(axis)
    return lax.ppermute(value, axis, [(source, source + steps) for source in range(count - steps)])


def shards(samples, pair_offsets, spectral_slot_position):
    devices = lax.axis_size("win")
    place = lax.axis_index("win")
    relative = whitened_slabs(
        samples, spectral_slot_position, place.reshape(1).astype(jnp.int32), devices
    )
    own = [relative[0]]
    for turn in range(1, devices):
        own.append(lax.ppermute(relative[turn], "win", [(s, s ^ turn) for s in range(devices)]))
    scale = 1.0 / (devices * samples.shape[0])
    offsets = pair_offsets[0]
    slots = offsets.shape[0]
    stacked = jnp.stack(own)
    farther = passed_along(stacked, "chan", 2)
    nearer = passed_along(stacked, "chan", 1)
    result = None
    for distance, partner in enumerate((own, nearer, farther)):
        slot = jnp.sum(jnp.where(offsets == distance, jnp.arange(slots), 0)).reshape(1).astype(jnp.int32)
        result = correlated(slot, own, [partner[n] for n in range(devices)], scale, result, slots)
    return result


def solution(mesh):
    in_specs = (P("win", "chan", None), P("chan", None), P())
    out_specs = P("chan", None, None, None, "win")
    return jax.shard_map(shards, mesh=mesh, in_specs=in_specs, out_specs=out_specs, check_vma=False)
```

```python
import functools
import math

import jax
import jax.numpy as jnp
import numpy as np
from jax import lax
from jax.experimental import pallas as pl
from jax.experimental.pallas import tpu as pltpu
from jax.sharding import PartitionSpec as P

HALF = 64
EPSILON = 1e-06
LANES = 128


def turned(value, numerator, denominator):
    real, imag = value
    numerator %= denominator
    if numerator == 0:
        return value
    if 2 * numerator == denominator:
        return (-real, None if imag is None else -imag)
    if 4 * numerator == denominator:
        return (imag, -real)
    if 4 * numerator == 3 * denominator:
        return (None if imag is None else -imag, real)
    c = math.cos(2 * math.pi * numerator / denominator)
    s = math.sin(2 * math.pi * numerator / denominator)
    if imag is None:
        return (real * c, real * (-s))
    return (real * c + imag * s, imag * c - real * s)


def plus(left, right):
    return tuple(b if a is None else a if b is None else a + b for a, b in zip(left, right))


def minus(left, right):
    return tuple(
        (None if b is None else -b) if a is None else a if b is None else a - b
        for a, b in zip(left, right)
    )


def scaled(value, factor):
    return tuple(None if a is None else a * factor for a in value)


def flipped(value):
    return (value[0], None if value[1] is None else -value[1])


def real_transform(count, first, stride, load):
    if count == 1:
        return [(load(first), None)]
    radix = 2 if count % 2 == 0 and count % 3 else 3 if count % 3 == 0 else count
    if radix == 2:
        part = count // 2
        even = real_transform(part, first, stride * 2, load)
        odd = real_transform(part, first + stride, stride * 2, load)
        bins = [None] * (count // 2 + 1)
        for k in range(part // 2 + 1):
            turn = turned(odd[k], k, count)
            bins[k] = plus(even[k], turn)
            if part - k != k:
                bins[part - k] = flipped(minus(even[k], turn))
        return bins
    if radix == 3:
        part = count // 3
        zero, one, two = (real_transform(part, first + stride * n, stride * 3, load) for n in range(3))
        bins = [None] * (count // 2 + 1)

        def keep(place, value):
            place %= count
            if place > count // 2:
                place, value = count - place, flipped(value)
            if bins[place] is None:
                bins[place] = value

        for k in range(part // 2 + 1):
            a, b = turned(one[k], k, count), turned(two[k], 2 * k, count)
            total, gap = plus(a, b), scaled(minus(a, b), math.sqrt(3.0) / 2)
            keep(k, plus(zero[k], total))
            middle = minus(zero[k], scaled(total, 0.5))
            side = turned(gap, 1, 4)
            keep(k + part, plus(middle, side))
            keep(k + 2 * part, minus(middle, side))
        return bins
    bins = []
    values = [(load(first + stride * n), None) for n in range(count)]
    for k in range(count // 2 + 1):
        bins.append(functools.reduce(plus, (turned(v, n * k, count) for n, v in enumerate(values))))
    return bins


def halves(value):
    high = value.astype(jnp.bfloat16)
    return high, (value - high.astype(jnp.float32)).astype(jnp.bfloat16)


@functools.lru_cache
def tables(span, half_width):
    outer = span // LANES
    lane = np.arange(LANES)
    turn = 2 * np.pi * np.outer(np.arange(outer // 2 + 1), lane) / span
    twiddles = np.stack([np.cos(turn), -np.sin(turn)], axis=1) / math.sqrt(span)
    inner = 2 * np.pi * (np.outer(lane, lane) % LANES) / LANES
    c, s = np.cos(inner), np.sin(inner)
    matrix = np.block([[c, -s], [s, c]]).astype(np.float32)
    high = matrix.astype(jnp.bfloat16)
    low = (matrix - high.astype(np.float32)).astype(jnp.bfloat16)
    gap = np.arange(4 * LANES)[:, None] - LANES - np.arange(2 * LANES)[None, :]
    band = (np.abs(gap) <= half_width).astype(jnp.bfloat16)
    return (
        twiddles.reshape(-1, LANES).astype(np.float32),
        np.stack([high, low]),
        band,
    )


def spectra_kernel(half_width, slab_count, place_ref, slot_ref, sample_ref, twiddle_ref, matrix_ref,
                   band_ref, *rest):
    out_refs = rest[:slab_count]
    high_ref, low_ref, fine_ref, spec_ref, power_ref = rest[slab_count:]
    windows, sensors, span = sample_ref.shape
    rows = windows * sensors
    freqs = slot_ref.shape[1]
    outer = span // LANES
    bins = outer // 2 + 1
    group = 16

    def outer_transform(step, carry):
        window = step // (sensors // group)
        start = pl.multiple_of((step % (sensors // group)) * group, group)
        first = pl.multiple_of(step * group, group)

        def load(place):
            piece = sample_ref[window, pl.ds(start, group), place * LANES:(place + 1) * LANES]
            return piece.astype(jnp.float32)

        for k, (real, imag) in enumerate(real_transform(outer, 0, 1, load)):
            c, s = twiddle_ref[2 * k:2 * k + 1, :], twiddle_ref[2 * k + 1:2 * k + 2, :]
            if imag is None:
                pair = (real * c, real * s)
            else:
                pair = (real * c - imag * s, real * s + imag * c)
            for part in range(2):
                high, low = halves(pair[part])
                high_ref[k, pl.ds(first, group), part * LANES:(part + 1) * LANES] = high
                low_ref[k, pl.ds(first, group), part * LANES:(part + 1) * LANES] = low
        return carry

    lax.fori_loop(0, rows // group, outer_transform, 0)

    high = high_ref[...].reshape(bins * rows, 2 * LANES)
    low = low_ref[...].reshape(bins * rows, 2 * LANES)
    fine = jnp.dot(high, matrix_ref[0], preferred_element_type=jnp.float32)
    fine += jnp.dot(low, matrix_ref[0], preferred_element_type=jnp.float32)
    fine += jnp.dot(high, matrix_ref[1], preferred_element_type=jnp.float32)
    fine_ref[...] = fine.reshape(bins, rows, 2 * LANES)

    def choose(block, carry):
        columns = pl.ds(pl.multiple_of(block * LANES, LANES), LANES)
        slot = slot_ref[:, columns].astype(jnp.float32)
        quotient = jnp.floor((slot + 0.5) * (1.0 / outer))
        remainder = slot - quotient * outer
        mirrored = remainder > outer // 2
        lane = jnp.where(mirrored, LANES - 1 - quotient, quotient).astype(jnp.int32)
        bin_index = jnp.where(mirrored, outer - remainder, remainder).astype(jnp.int32)
        lane = jnp.broadcast_to(lane, (8, LANES))
        bin_index = jnp.broadcast_to(bin_index, (8, LANES))
        sign = jnp.broadcast_to(jnp.where(mirrored, -1.0, 1.0), (8, LANES))
        chosen = [[jnp.zeros((8, LANES), jnp.float32)] * 2 for _ in range(rows // 8)]
        for k in range(bins):
            here = bin_index == k
            for r in range(rows // 8):
                for part in range(2):
                    piece = fine_ref[k, r * 8:(r + 1) * 8, part * LANES:(part + 1) * LANES]
                    moved = jnp.take_along_axis(piece, lane, axis=1)
                    chosen[r][part] = jnp.where(here, moved, chosen[r][part])
        for r in range(rows // 8):
            real, imag = chosen[r][0], chosen[r][1] * sign
            spec_ref[0, r * 8:(r + 1) * 8, columns] = real
            spec_ref[1, r * 8:(r + 1) * 8, columns] = imag
            power_ref[r * 8:(r + 1) * 8, columns] = real * real + imag * imag
        return carry

    lax.fori_loop(0, freqs // LANES, choose, 0)

    high, low = halves(power_ref[...])
    both = jnp.concatenate([high, low], axis=0)
    width = 2 * LANES
    place = place_ref[0]
    slab = freqs // slab_count
    smooth = []
    for c in range(freqs // width):
        first, last = max(0, c * width - LANES), min(freqs, (c + 1) * width + LANES)
        offset = first - (c * width - LANES)
        total = jnp.dot(both[:, first:last], band_ref[offset:offset + last - first, :],
                        preferred_element_type=jnp.float32)
        total = total[:rows] + total[rows:]
        spot = lax.broadcasted_iota(jnp.int32, (1, width), 1) + c * width
        tally = jnp.minimum(spot + half_width, freqs - 1) - jnp.maximum(spot - half_width, 0) + 1
        factor = lax.rsqrt(total / tally.astype(jnp.float32) + EPSILON)
        for part in range(2):
            spec_ref[part, :, c * width:(c + 1) * width] *= factor
    for turn, out_ref in enumerate(out_refs):
        columns = pl.ds(pl.multiple_of((place ^ turn) * slab, LANES), slab)
        for window in range(windows):
            for part in range(2):
                out_ref[window, part] = spec_ref[part, window * sensors:(window + 1) * sensors, columns]


def whitened_slabs(samples, slots, place, slab_count):
    windows, sensors, span = samples.shape
    freqs = slots.shape[0]
    rows = windows * sensors
    bins = span // LANES // 2 + 1
    twiddles, matrix, band = tables(span, HALF)
    whole = pl.BlockSpec(memory_space=pltpu.VMEM)
    return pl.pallas_call(
        functools.partial(spectra_kernel, HALF, slab_count),
        out_shape=[
            jax.ShapeDtypeStruct((windows, 2, sensors, freqs // slab_count), jnp.float32)
        ] * slab_count,
        in_specs=[pl.BlockSpec(memory_space=pltpu.SMEM)] + [whole] * 5,
        out_specs=[whole] * slab_count,
        scratch_shapes=[
            pltpu.VMEM((bins, rows, 2 * LANES), jnp.bfloat16),
            pltpu.VMEM((bins, rows, 2 * LANES), jnp.bfloat16),
            pltpu.VMEM((bins, rows, 2 * LANES), jnp.float32),
            pltpu.VMEM((2, rows, freqs), jnp.float32),
            pltpu.VMEM((rows, freqs), jnp.float32),
        ],
        name="whitened_slabs",
    )(place, slots.reshape(1, freqs), samples, jnp.asarray(twiddles), jnp.asarray(matrix), jnp.asarray(band))


def correlate_kernel(count, last, slot_ref, scale_ref, *rest):
    mine, partner = rest[:count], rest[count:2 * count]
    out_ref, left_ref, right_ref = rest[-3:]
    earlier_ref = rest[2 * count] if len(rest) > 2 * count + 3 + last else None
    windows = mine[0].shape[0]
    block = out_ref.shape[0]
    sensors, freqs = mine[0].shape[-2:]
    base = pl.program_id(0) * block

    @pl.when(pl.program_id(0) == 0)
    def prepare():
        scale = scale_ref[0]
        for n in range(count):
            for w in range(windows):
                for c in range(freqs // LANES):
                    columns = slice(c * LANES, (c + 1) * LANES)
                    real, imag = (mine[n][w, p, :, columns] * scale for p in range(2))
                    left_ref[n * windows + w, 0, c] = real + imag
                    left_ref[n * windows + w, 1, c] = real
                    left_ref[n * windows + w, 2, c] = imag
                real, imag = partner[n][w, 0], partner[n][w, 1]
                right_ref[n * windows + w, 0] = real
                right_ref[n * windows + w, 1] = real + imag
                right_ref[n * windows + w, 2] = imag - real

    def one(step, carry):
        for c in range(freqs // LANES):
            columns = slice(c * LANES, (c + 1) * LANES)
            left = [
                [
                    jnp.broadcast_to(left_ref[w, p, c, pl.ds(base + step, 1)], (8, LANES))
                    for p in range(3)
                ]
                for w in range(count * windows)
            ]
            for g in range(sensors // 8):
                lines = slice(g * 8, (g + 1) * 8)
                sums = [
                    functools.reduce(
                        lambda x, y: x + y,
                        [left[w][p] * right_ref[w, p, lines, columns] for w in range(count * windows)],
                    )
                    for p in range(3)
                ]
                real, imag = sums[0] + sums[2], sums[0] - sums[1]
                if earlier_ref is not None:
                    real += earlier_ref[step, 0, lines, columns]
                    imag += earlier_ref[step, 1, lines, columns]
                if last:
                    out_ref[step, 0, 0, lines, columns] = real
                    out_ref[step, 0, 1, lines, columns] = imag
                else:
                    out_ref[step, 0, lines, columns] = real
                    out_ref[step, 1, lines, columns] = imag
        return carry

    lax.fori_loop(0, block, one, 0)


def correlated(slot, scale, mine, partner, earlier, result, slots):
    windows, _, sensors, freqs = mine[0].shape
    block = 4 if sensors % 4 == 0 else 1
    count = len(mine)
    last = slots is not None
    whole = pl.BlockSpec(mine[0].shape, lambda i, slot: (0, 0, 0, 0))
    part_spec = pl.BlockSpec((block, 2, sensors, freqs), lambda i, slot: (i, 0, 0, 0))
    operands = list(mine) + list(partner)
    in_specs = [pl.BlockSpec(memory_space=pltpu.SMEM)] + [whole] * len(operands)
    aliases = {}
    if earlier is not None:
        operands.append(earlier)
        in_specs.append(part_spec)
    if last:
        out_shape = jax.ShapeDtypeStruct((sensors, slots, 2, sensors, freqs), jnp.float32)
        out_spec = pl.BlockSpec((block, 1, 2, sensors, freqs), lambda i, slot: (i, slot[0], 0, 0, 0))
        if result is None:
            result = jnp.zeros((1, 1), jnp.float32)
        else:
            aliases = {2 + len(operands): 0}
        operands.append(result)
        in_specs.append(pl.BlockSpec(memory_space=pl.ANY))
    else:
        out_shape = jax.ShapeDtypeStruct((sensors, 2, sensors, freqs), jnp.float32)
        out_spec = part_spec
    return pl.pallas_call(
        functools.partial(correlate_kernel, count, last),
        out_shape=out_shape,
        grid_spec=pltpu.PrefetchScalarGridSpec(
            num_scalar_prefetch=1,
            grid=(sensors // block,),
            in_specs=in_specs,
            out_specs=out_spec,
            scratch_shapes=[
                pltpu.VMEM((count * windows, 3, freqs // LANES, sensors, LANES), jnp.float32),
                pltpu.VMEM((count * windows, 3, sensors, freqs), jnp.float32),
            ],
        ),
        input_output_aliases=aliases,
        cost_estimate=pl.CostEstimate(
            flops=8 * count * windows * sensors * sensors * freqs,
            bytes_accessed=8 * sensors * sensors * freqs,
            transcendentals=0,
        ),
        name="correlated",
    )(slot, scale, *operands)


def shards(samples, pair_offsets, spectral_slot_position):
    devices, blocks = lax.axis_size("win"), lax.axis_size("chan")
    place, block = lax.axis_index("win"), lax.axis_index("chan")
    relative = whitened_slabs(
        samples, spectral_slot_position, place.reshape(1).astype(jnp.int32), devices
    )
    own = [relative[0]]
    for turn in range(1, devices):
        own.append(lax.ppermute(relative[turn], "win", [(s, s ^ turn) for s in range(devices)]))
    half = max(1, devices // 2)
    own = [jnp.concatenate(own[n:n + half]) for n in range(0, devices, half)]

    def ring(value, steps):
        return lax.ppermute(value, "chan", [(s, (s + steps) % blocks) for s in range(blocks)])

    farther, nearer = [], []
    for piece in own:
        far = ring(piece, 2)
        farther.append(far)
        if blocks % 2:
            nearer.append(ring(piece, 1))
        else:
            passed = jnp.where(block % 2 == 1, far, piece)
            nearer.append(lax.ppermute(passed, "chan", [(s, s ^ 1) for s in range(blocks)]))

    offsets = pair_offsets[0]
    slots = offsets.shape[0]
    distances = jnp.arange(3)
    targets = jnp.sum(jnp.where(offsets[None, :] == distances[:, None], jnp.arange(slots), 0), axis=1)
    targets = targets.astype(jnp.int32)
    scales = jnp.where(block >= distances, 1.0 / (devices * samples.shape[0]), 0.0).astype(jnp.float32)

    def slot_of(distance):
        return targets[distance:distance + 1], scales[distance:distance + 1]

    result = None
    partial = correlated(*slot_of(0), own[:1], own[:1], None, None, None)
    result = correlated(*slot_of(0), own[1:], own[1:], partial, result, slots)
    result = correlated(*slot_of(2), own, farther, None, result, slots)
    partial = correlated(*slot_of(1), own[:1], nearer[:1], None, None, None)
    return correlated(*slot_of(1), own[1:], nearer[1:], partial, result, slots)


def solution(mesh):
    in_specs = (P("win", "chan", None), P("chan", None), P())
    out_specs = P("chan", None, None, None, "win")
    return jax.shard_map(shards, mesh=mesh, in_specs=in_specs, out_specs=out_specs, check_vma=False)
```
